256 devices in a mesh: pipe: 8 (over y, core), expert: 32 (over z, x).
Axes of the slice: x: 4, y: 4, z: 8, core: 2. Of those that a mesh axis runs over, the one named last changes fastest.
Arguments:
- layer_input: bfloat16 [8, 2048, 2880], P('pipe', 'expert'), may hold values from -6 to 6
- grad_output: bfloat16 [8, 2048, 2880], P('pipe', 'expert'), may hold values from -6 to 6
- expert_ids: int32 [8, 2048, 4], P('pipe', 'expert'), may hold values from 0 to 127, as said below
- gate_probs: float32 [8, 2048, 4], P('pipe', 'expert'), may hold values from 0.05 to 1
- w_gate: bfloat16 [8, 11520, 2880], P('pipe', 'expert'), may hold values from -0.109375 to 0.109375
- w_up: bfloat16 [8, 11520, 2880], P('pipe', 'expert'), may hold values from -0.109375 to 0.109375
- w_down: bfloat16 [8, 11520, 2880], P('pipe', 'expert'), may hold values from -0.109375 to 0.109375
Outputs:
- grad_gate: bfloat16 [8, 11520, 2880], P('pipe', 'expert')
- grad_up: bfloat16 [8, 11520, 2880], P('pipe', 'expert')
- grad_down: bfloat16 [8, 11520, 2880], P('pipe', 'expert')
- grad_prev: bfloat16 [8, 2048, 2880], P('pipe', 'expert')
The draws below stay inside these ranges and needn't reach their ends.
Inputs may be any that keep to these rules, and one draw needn't show every extreme that they name: `expert_ids`: in each section, within the 64 tokens of one device, no expert is named by more than 4 tokens; in each section one expert below 4, the same for all devices of that section, is named by exactly 4 tokens of every device; a token names 4 different experts.
All inputs are finite; a program needn't handle non-finite values.
Results may differ from the reference program's by a relative error of at most 0.0085.
Values may be sent and summed in bfloat16 or wider, within the bound.
A program may use at most 64 MiB of HBM per device.

```python
import math
from functools import partial
import jax
import jax.numpy as jnp
from jax import lax

D = 2880
FF = 2880
EXPERTS = 128
TOPK = 4
SLICES = 8
TOK_DEV = 64
CAP = 4
HS = 360
FLIGHT = 4
TOKENS = 2048
N_PIPE = 8


def route_block(block_key, shifts):
    jitter_key, order_key, token_key = jax.random.split(block_key, 3)
    tickets = EXPERTS * CAP
    jitter = jax.random.randint(jitter_key, (EXPERTS, CAP), 0, 65536).astype(jnp.int32)
    scores = (shifts[:, None] + jitter) * tickets + jnp.arange(tickets, dtype=jnp.int32).reshape(EXPERTS, CAP)
    values_top, picked = lax.top_k(scores.reshape(tickets), TOK_DEV * TOPK)
    picked = picked.astype(jnp.int32)
    owners = picked // CAP
    within = picked % CAP
    shuffled = jax.random.permutation(order_key, EXPERTS).astype(jnp.int32)
    position = jnp.argsort(shuffled, stable=True).astype(jnp.int32)
    arranged = owners[jnp.argsort(position[owners] * CAP + within, stable=True)]
    layout = arranged.reshape(TOPK, TOK_DEV).T
    return layout[jax.random.permutation(token_key, TOK_DEV)]


def route_section(section_key):
    level_key, favored_key, rest_key = jax.random.split(section_key, 3)
    blocks = TOKENS // TOK_DEV
    levels = jax.random.randint(level_key, (EXPERTS,), 0, 4).astype(jnp.int32)
    favored = jax.random.randint(favored_key, (), 0, FLIGHT).astype(jnp.int32)
    shifts = jnp.where(jnp.arange(EXPERTS, dtype=jnp.int32) == favored, 262144, levels * 16384).astype(jnp.int32)
    block_keys = jax.random.split(rest_key, blocks)
    routed = jax.vmap(partial(route_block, shifts=shifts))(block_keys)
    return routed.reshape(blocks * TOK_DEV, TOPK)


def draw_expert_ids(key, part):
    folded = jax.random.fold_in(key, 7)
    section_keys = jax.random.split(folded, N_PIPE)
    return jax.vmap(route_section)(section_keys).astype(jnp.int32)


def block_scale(rng, dims, cuts, low, high):
    def one(dim, parts):
        steps = jax.random.uniform(jax.random.fold_in(jax.random.fold_in(rng, 6), dim), (parts,), jnp.float32, low / len(cuts), high / len(cuts))
        return jnp.repeat(jnp.exp(steps), dims[dim] // parts).reshape((-1,) + (1,) * (len(dims) - dim - 1))

    loudness = one(*cuts[0])
    for cut in cuts[1:]:
        loudness = loudness * one(*cut)
    return loudness


def bell_draw(stream_key, shape, scale, limit, pieces=(), kind=jnp.bfloat16):
    result = scale * jax.random.normal(stream_key, shape, jnp.float32)
    if pieces:
        result = result * block_scale(stream_key, shape, pieces, -0.22, 0.18)
    return jnp.clip(result, -limit, limit).astype(kind)


def setup_inputs(seed: int = 0) -> dict:
    keys = jax.random.split(jax.random.key(seed), 8)
    layer_input = bell_draw(keys[0], (N_PIPE, TOKENS, D), 1.0, 6.0, ((0, 8), (1, 32)))
    grad_output = bell_draw(keys[1], (N_PIPE, TOKENS, D), 1.0, 6.0, ((0, 8), (1, 32)))
    expert_ids = draw_expert_ids(jax.random.fold_in(keys[7], 71), 0)
    gate_probs = jnp.clip(jnp.exp(math.log(1.0) - 2.9957323 * jax.random.uniform(keys[3], (N_PIPE, TOKENS, TOPK), jnp.float32) ** block_scale(keys[3], (N_PIPE, TOKENS, TOPK), ((0, 8), (1, 32)), -0.2, 0.2)), 0.05, 1.0)
    w_gate = bell_draw(keys[4], (N_PIPE, FLIGHT * FF, D), D ** -0.5, 0.109375, ((0, 8), (1, 32)))
    w_up = bell_draw(keys[5], (N_PIPE, FLIGHT * FF, D), D ** -0.5, 0.109375, ((0, 8), (1, 32)))
    w_down = bell_draw(keys[6], (N_PIPE, FLIGHT * FF, D), FF ** -0.5, 0.109375, ((0, 8), (1, 32)))
    return {"layer_input": layer_input, "grad_output": grad_output, "expert_ids": expert_ids, "gate_probs": gate_probs, "w_gate": w_gate, "w_up": w_up, "w_down": w_down}


def silu_parts(pre_gate):
    sigma = jax.nn.sigmoid(pre_gate)
    return pre_gate * sigma, sigma * (1.0 + pre_gate * (1.0 - sigma))


def contract_first(left, right):
    return lax.dot_general(left, right, (((0,), (0,)), ((), ())), preferred_element_type=jnp.float32)


def contract_last(left, right):
    return lax.dot_general(left, right, (((1,), (1,)), ((), ())), preferred_element_type=jnp.float32)


def reference(layer_input, grad_output, expert_ids, gate_probs, w_gate, w_up, w_down):
    sections = layer_input.shape[0]
    total = layer_input.shape[1]
    flight = w_gate.shape[1] // FF
    blocks = total // TOK_DEV
    buffer_rows = blocks * CAP
    gate_all, up_all, down_all, input_all = [], [], [], []
    for section in range(sections):
        inputs = layer_input[section]
        cotan = grad_output[section]
        scaled = (gate_probs[section][:, :, None] * cotan[:, None, :].astype(jnp.float32)).astype(jnp.bfloat16)
        input_grad = jnp.zeros((total, D), jnp.float32)
        gate_list, up_list, down_list = [], [], []
        for expert in range(flight):
            matched = expert_ids[section] == expert
            hit = jnp.any(matched, axis=1)
            picked = jnp.sum(jnp.where(matched[:, :, None], scaled.astype(jnp.float32), 0.0), axis=1).astype(jnp.bfloat16)
            hit_int = hit.astype(jnp.int32).reshape(blocks, TOK_DEV)
            ranks = jnp.cumsum(hit_int, axis=1) - 1
            base = (jnp.arange(blocks, dtype=jnp.int32) * CAP)[:, None]
            target = jnp.where(hit_int > 0, base + ranks, buffer_rows).reshape(total).astype(jnp.int32)
            in_rows = jnp.zeros((buffer_rows, D), jnp.bfloat16).at[target].set(inputs, mode="drop")
            co_rows = jnp.zeros((buffer_rows, D), jnp.bfloat16).at[target].set(picked, mode="drop")
            weight_gate = w_gate[section, expert * FF:(expert + 1) * FF]
            weight_up = w_up[section, expert * FF:(expert + 1) * FF]
            weight_down = w_down[section, expert * FF:(expert + 1) * FF]
            pre_gate = contract_last(in_rows, weight_gate)
            pre_up = contract_last(in_rows, weight_up)
            silu_val, silu_grad = silu_parts(pre_gate)
            hidden = (silu_val * pre_up).astype(jnp.bfloat16)
            hidden_grad = contract_last(co_rows, weight_down)
            grad_pre_gate = (hidden_grad * pre_up * silu_grad).astype(jnp.bfloat16)
            grad_pre_up = (hidden_grad * silu_val).astype(jnp.bfloat16)
            down_list.append(contract_first(hidden, co_rows).astype(jnp.bfloat16))
            gate_list.append(contract_first(grad_pre_gate, in_rows).astype(jnp.bfloat16))
            up_list.append(contract_first(grad_pre_up, in_rows).astype(jnp.bfloat16))
            partial_value = jnp.einsum("rsh,shd->rsd", grad_pre_gate.astype(jnp.float32).reshape(buffer_rows, SLICES, HS),
                                 weight_gate.astype(jnp.float32).reshape(SLICES, HS, D), precision=lax.Precision.HIGHEST)
            partial_value = partial_value + jnp.einsum("rsh,shd->rsd", grad_pre_up.astype(jnp.float32).reshape(buffer_rows, SLICES, HS),
                                           weight_up.astype(jnp.float32).reshape(SLICES, HS, D), precision=lax.Precision.HIGHEST)
            combined = jnp.sum(partial_value.astype(jnp.bfloat16).astype(jnp.float32), axis=1)
            safe_target = jnp.minimum(target, buffer_rows - 1)
            input_grad = input_grad + jnp.where(hit[:, None], combined[safe_target], 0.0)
        gate_all.append(jnp.concatenate(gate_list, axis=0))
        up_all.append(jnp.concatenate(up_list, axis=0))
        down_all.append(jnp.concatenate(down_list, axis=0))
        input_all.append(input_grad.astype(jnp.bfloat16))
    shifted = input_all[1:] + [jnp.zeros((total, D), jnp.bfloat16)]
    return jnp.stack(gate_all), jnp.stack(up_all), jnp.stack(down_all), jnp.stack(shifted)
```

```python
import jax
import jax.numpy as jnp
from jax import lax
from jax.experimental import pallas as pl
from jax.experimental.pallas import tpu as pltpu
from jax.sharding import PartitionSpec as P

D = 2880
HS = 360
TOK = 64
FLIGHT = 4
NX = 4
NZ = 8
HALF = 1408
WIDE = D - HALF
CHUNKS = ((0, 768), (768, WIDE))
ARRIVAL = (0, 1, 7, 2, 6, 3, 5, 4)
LAG = 3
MESH = pl.DeviceIdType.MESH
F32 = jnp.float32
BF16 = jnp.bfloat16


def nt(left, right):
    return lax.dot_general(left, right, (((1,), (1,)), ((), ())), preferred_element_type=F32)


def nn(left, right):
    return jnp.dot(left, right, preferred_element_type=F32)


def selector(ids, rows, per_expert):
    row = lax.broadcasted_iota(jnp.int32, (rows, TOK), 0)
    owner = row // per_expert
    matches = [ids[k : k + 1, :] == owner for k in range(4)]
    hit = matches[0] | matches[1] | matches[2] | matches[3]
    before = lax.broadcasted_iota(jnp.int32, (TOK, TOK), 0)
    token = lax.broadcasted_iota(jnp.int32, (TOK, TOK), 1)
    earlier = jnp.where(before < token, 1.0, 0.0).astype(BF16)
    rank = nn(jnp.where(hit, 1.0, 0.0).astype(BF16), earlier)
    return jnp.where(hit & (rank == (row % 4).astype(F32)), 1.0, 0.0), matches, row % 8 < 4


def kernel(
    x_hbm, g_hbm, ids_hbm, pr_hbm, wg_hbm, wu_hbm, wd_hbm,
    gg_hbm, gu_hbm, gd_hbm, gp_hbm,
    x_v, g_v, ids_v, ids2_v, pr_v, wg_v, wu_v, wd_v, send_v, rows_v,
    part_v, gg_v, gu_v, gd_v, gp_v,
    q1a, q1b, q2a, q2b, ta, tb, fa, fb,
    lsem, osem, sem_z, sem_x, sem_f, sem_r, sem_ids, s1, r1, s2, r2, s3, r3,
):
    pipe = lax.axis_index("pipe")
    me = lax.axis_index("expert")
    z = lax.div(me, NX)
    x = lax.rem(me, NX)
    xr = lax.rem(x + 1, NX)
    xl = lax.rem(x + NX - 1, NX)
    xo = lax.rem(x + 2, NX)

    def same(zz, xx):
        return {"pipe": pipe, "expert": zz * NX + xx}

    loads = [
        pltpu.make_async_copy(src.at[0], dst, lsem.at[i])
        for i, (src, dst) in enumerate(
            (
                (ids_hbm, ids_v),
                (pr_hbm, pr_v),
                (x_hbm, x_v),
                (g_hbm, g_v),
                (wg_hbm, wg_v),
                (wu_hbm, wu_v),
                (wd_hbm, wd_v),
            )
        )
    ]
    for load in loads:
        load.start()

    barrier = pltpu.get_barrier_semaphore()
    for d in range(1, NZ):
        pl.semaphore_signal(barrier, 1, device_id=same(lax.rem(z + d, NZ), x), device_id_type=MESH)
    for xn in (xl, xr):
        pl.semaphore_signal(barrier, 1, device_id=same(z, xn), device_id_type=MESH)

    @pl.when(pipe > 0)
    def _():
        for d in range(NZ):
            pl.semaphore_signal(
                barrier, 1, device_id={"pipe": pipe - 1, "expert": lax.rem(z + d, NZ) * NX + x},
                device_id_type=MESH,
            )

    @pl.when(pipe < 7)
    def _():
        for d in range(NZ):
            pl.semaphore_signal(
                barrier, 1, device_id={"pipe": pipe + 1, "expert": lax.rem(z + d, NZ) * NX + x},
                device_id_type=MESH,
            )

    loads[0].wait()
    loads[1].wait()
    ids = ids_v[...]
    sel, matches, is_in = selector(ids, 32, 8)
    probs = pr_v[...]
    weight = jnp.zeros((32, TOK), F32)
    for k in range(4):
        weight = weight + jnp.where(matches[k], probs[k : k + 1, :], 0.0)
    weight_col = jnp.sum(weight * sel, axis=1, keepdims=True)
    sel_in = jnp.where(is_in, sel, 0.0).astype(BF16)
    sel_co = jnp.where(is_in, 0.0, sel).astype(BF16)
    loads[2].wait()
    loads[3].wait()
    picked = nn(sel_in, x_v[...]) + nn(sel_co, g_v[...]) * weight_col
    send_v[...] = picked.reshape(FLIGHT, 8, D).astype(BF16)

    pl.semaphore_wait(barrier, jnp.where((pipe == 0) | (pipe == 7), 17, 25))

    def block(xs, d):
        return (xs, lax.rem(z + NZ - d, NZ))

    own = pltpu.make_async_copy(send_v.at[lax.div(z, 2)], rows_v.at[x, z], sem_r.at[x, z])
    own.start()
    z_sends = []
    for d in ARRIVAL[1:]:
        zt = lax.rem(z + d, NZ)
        z_sends.append(
            pltpu.make_async_remote_copy(
                send_v.at[lax.div(zt, 2)], rows_v.at[x, z], sem_z.at[d], sem_r.at[x, z],
                device_id=same(zt, x), device_id_type=MESH,
            )
        )
        z_sends[-1].start()

    @pl.when(pipe > 0)
    def _():
        pltpu.make_async_remote_copy(
            ids_v, ids2_v, sem_ids.at[0], sem_ids.at[1],
            device_id={"pipe": pipe - 1, "expert": me}, device_id_type=MESH,
        ).start()

    def arrived(xs, d):
        b = block(xs, d)
        return pltpu.make_async_remote_copy(
            rows_v.at[b], rows_v.at[b], sem_z.at[0], sem_r.at[b],
            device_id=same(z, xr), device_id_type=MESH,
        )

    x_sends = []

    def push(xs, d, to, sem):
        b = block(xs, d)
        x_sends.append(
            pltpu.make_async_remote_copy(
                rows_v.at[b], rows_v.at[b], sem, sem_r.at[b], device_id=same(z, to), device_id_type=MESH
            )
        )
        x_sends[-1].start()

    def forward(d):
        arrived(xl, d).wait_recv()
        arrived(xr, d).wait_recv()
        if d % 2 == 0:
            push(xl, d, xr, sem_f.at[d])
        else:
            push(xr, d, xl, sem_f.at[d])

    for i, d in enumerate(ARRIVAL):
        if d == 0:
            own.wait()
        else:
            arrived(x, d).wait_recv()
        push(x, d, xr, sem_x.at[0, d])
        push(x, d, xl, sem_x.at[1, d])
        if i >= LAG:
            forward(ARRIVAL[i - LAG])
    for d in ARRIVAL[NZ - LAG :]:
        forward(d)
    for load in loads[4:]:
        load.wait()
    for d in ARRIVAL:
        arrived(xo, d).wait_recv()

    rows = rows_v[...].reshape(256, D)
    pre_gate = nt(wg_v[...], rows)
    pre_up = nt(wu_v[...], rows)
    hidden_grad = pltpu.roll(nt(wd_v[...], rows), 252, 1)
    in_col = lax.broadcasted_iota(jnp.int32, (HS, 256), 1) % 8 < 4
    sigma = jax.nn.sigmoid(pre_gate)
    silu = pre_gate * sigma
    slope = sigma * (1.0 + pre_gate * (1.0 - sigma))
    hidden = jnp.where(in_col, silu * pre_up, 0.0)
    d_gate = jnp.where(in_col, hidden_grad * pre_up * slope, 0.0)
    d_up = jnp.where(in_col, hidden_grad * silu, 0.0)
    hidden_co = pltpu.roll(hidden, 4, 1).astype(BF16)
    gate_lo = d_gate.T.astype(BF16)
    up_lo = d_up.T.astype(BF16)
    gate_hi = pltpu.roll(d_gate, 4, 1).T.astype(BF16)
    up_hi = pltpu.roll(d_up, 4, 1).T.astype(BF16)
    d_gate = d_gate.astype(BF16)
    d_up = d_up.astype(BF16)

    mate = x + 1 - 2 * lax.rem(x, 2)
    far = NX - 1 - x
    mates = ((mate, far), (far, mate))
    q1s, q2s, ts, fs = (q1a, q1b), (q2a, q2b), (ta, tb), (fa, fb)
    tail = []

    def step1(k):
        c0, c1 = CHUNKS[k]
        first, _ = mates[k]
        other = NX - 1 - first if k == 0 else first + 1 - 2 * lax.rem(first, 2)
        out = []
        for slot, dest in enumerate((first, other)):
            out.append(
                pltpu.make_async_remote_copy(
                    part_v.at[dest, :, pl.ds(c0, c1 - c0)], q1s[k].at[slot], s1.at[k, slot], r1.at[k, slot],
                    device_id=same(z, first), device_id_type=MESH,
                )
            )
        return out

    def step2(k):
        c0, c1 = CHUNKS[k]
        _, second = mates[k]
        return pltpu.make_async_remote_copy(
            part_v.at[second, :, pl.ds(c0, c1 - c0)], q2s[k], s2.at[k], r2.at[k],
            device_id=same(z, second), device_id_type=MESH,
        )

    def step3(k, d):
        zt = lax.rem(z + d, NZ)
        return pltpu.make_async_remote_copy(
            ts[k].at[zt], fs[k].at[z], s3.at[k, d], r3.at[k, z],
            device_id={"pipe": pipe - 1, "expert": zt * NX + x}, device_id_type=MESH,
        )

    def partials(k):
        c0, c1 = CHUNKS[k]
        lo1 = min(c1, HALF)
        low = nn(gate_lo, wg_v[:, c0:lo1]) + nn(up_lo, wu_v[:, c0:lo1])
        high = nn(gate_hi, wg_v[:, HALF + c0 : HALF + c1]) + nn(up_hi, wu_v[:, HALF + c0 : HALF + c1])
        part_v[:, :, c0:lo1] = (low + high[:, : lo1 - c0]).astype(BF16).reshape(NX, 64, lo1 - c0)
        if c1 > lo1:
            part_v[:, :, lo1:c1] = high[:, lo1 - c0 :].astype(BF16).reshape(NX, 64, c1 - lo1)
        for copy in step1(k):
            copy.start()

    def reduce1(k):
        c0, c1 = CHUNKS[k]
        _, second = mates[k]
        for copy in step1(k):
            copy.wait_recv()
        part_v[second, :, c0:c1] = (
            part_v[second, :, c0:c1].astype(F32) + q1s[k][1].astype(F32)
        ).astype(BF16)
        step2(k).start()

    def reduce2(k):
        c0, c1 = CHUNKS[k]
        step2(k).wait_recv()
        total = (
            part_v[x, :, c0:c1].astype(F32) + q1s[k][0].astype(F32) + q2s[k][...].astype(F32)
        )
        ts[k][...] = total.reshape(NZ, 8, c1 - c0).astype(BF16)

        @pl.when(pipe > 0)
        def _():
            for d in range(NZ):
                step3(k, d).start()

    stores = []

    def grads(left, out_v, out_hbm, sem):
        for c0 in range(0, D, 576 * 5):
            c1 = min(c0 + 576 * 5, D)
            cols = rows_v[:, :, :, c0:c1].reshape(256, c1 - c0)
            out_v[:, c0:c1] = nn(left, cols).astype(BF16)
        stores.append(pltpu.make_async_copy(out_v, out_hbm.at[0], sem))
        stores[-1].start()

    partials(0)
    partials(1)
    grads(hidden_co, gd_v, gd_hbm, osem.at[0])
    reduce1(0)
    reduce1(1)
    grads(d_gate, gg_v, gg_hbm, osem.at[1])
    reduce2(0)
    reduce2(1)
    grads(d_up, gu_v, gu_hbm, osem.at[2])

    @pl.when(pipe == 7)
    def _():
        gp_v[...] = jnp.zeros_like(gp_v)

    @pl.when(pipe < 7)
    def _():
        pltpu.make_async_remote_copy(
            ids_v, ids2_v, sem_ids.at[0], sem_ids.at[1],
            device_id={"pipe": pipe, "expert": me}, device_id_type=MESH,
        ).wait_recv()
        sel2, _, low_half = selector(ids2_v[...], 64, 16)
        sel_lo = jnp.where(low_half, sel2, 0.0).T.astype(BF16)
        sel_hi = jnp.where(low_half, 0.0, sel2).T.astype(BF16)
        for k, (c0, c1) in enumerate(CHUNKS):
            for d in range(NZ):
                zs = lax.rem(z + d, NZ)
                pltpu.make_async_remote_copy(
                    ts[k].at[0], fs[k].at[zs], s3.at[k, 0], r3.at[k, zs],
                    device_id={"pipe": pipe, "expert": me}, device_id_type=MESH,
                ).wait_recv()
            got = fs[k][...].reshape(64, c1 - c0)
            lo1 = min(c1, HALF)
            gp_v[:, c0:lo1] = nn(sel_lo, got[:, : lo1 - c0]).astype(BF16)
            gp_v[:, HALF + c0 : HALF + c1] = nn(sel_hi, got).astype(BF16)

    last = pltpu.make_async_copy(gp_v, gp_hbm.at[0], osem.at[3])
    last.start()

    for copy in z_sends + x_sends:
        copy.wait_send()
    for k in range(2):
        for copy in step1(k):
            copy.wait_send()
        step2(k).wait_send()

    @pl.when(pipe > 0)
    def _():
        pltpu.make_async_remote_copy(
            ids_v, ids2_v, sem_ids.at[0], sem_ids.at[1],
            device_id={"pipe": pipe - 1, "expert": me}, device_id_type=MESH,
        ).wait_send()
        for k in range(2):
            for d in range(NZ):
                step3(k, d).wait_send()

    for store in stores:
        store.wait()
    last.wait()


def body(layer_input, grad_output, expert_ids, gate_probs, w_gate, w_up, w_down):
    ids = jnp.transpose(expert_ids, (0, 2, 1))
    probs = jnp.transpose(gate_probs, (0, 2, 1))
    dma = pltpu.SemaphoreType.DMA
    w0, w1 = (c1 - c0 for c0, c1 in CHUNKS)
    wide = (HS, D)
    return tuple(pl.pallas_call(
        kernel,
        out_shape=[jax.ShapeDtypeStruct((1, HS, D), BF16)] * 3 + [jax.ShapeDtypeStruct((1, TOK, D), BF16)],
        in_specs=[pl.BlockSpec(memory_space=pl.ANY)] * 7,
        out_specs=[pl.BlockSpec(memory_space=pl.ANY)] * 4,
        scratch_shapes=[
            pltpu.VMEM((TOK, D), BF16),
            pltpu.VMEM((TOK, D), BF16),
            pltpu.VMEM((4, TOK), jnp.int32),
            pltpu.VMEM((4, TOK), jnp.int32),
            pltpu.VMEM((4, TOK), F32),
            pltpu.VMEM(wide, BF16),
            pltpu.VMEM(wide, BF16),
            pltpu.VMEM(wide, BF16),
            pltpu.VMEM((FLIGHT, 8, D), BF16),
            pltpu.VMEM((NX, NZ, 8, D), BF16),
            pltpu.VMEM((NX, 64, WIDE), BF16),
            pltpu.VMEM(wide, BF16),
            pltpu.VMEM(wide, BF16),
            pltpu.VMEM(wide, BF16),
            pltpu.VMEM((TOK, D), BF16),
            pltpu.VMEM((2, 64, w0), BF16),
            pltpu.VMEM((2, 64, w1), BF16),
            pltpu.VMEM((64, w0), BF16),
            pltpu.VMEM((64, w1), BF16),
            pltpu.VMEM((NZ, 8, w0), BF16),
            pltpu.VMEM((NZ, 8, w1), BF16),
            pltpu.VMEM((NZ, 8, w0), BF16),
            pltpu.VMEM((NZ, 8, w1), BF16),
            dma((7,)),
            dma((4,)),
            dma((NZ,)),
            dma((2, NZ)),
            dma((NZ,)),
            dma((NX, NZ)),
            dma((2,)),
            dma((2, 2)),
            dma((2, 2)),
            dma((2,)),
            dma((2,)),
            dma((2, NZ)),
            dma((2, NZ)),
        ],
        compiler_params=pltpu.CompilerParams(
            collective_id=0, has_side_effects=True, vmem_limit_bytes=48 * 1024 * 1024
        ),
    )(layer_input, grad_output, ids, probs, w_gate, w_up, w_down))


def solution(mesh):
    spec = P("pipe", "expert", None)
    return jax.shard_map(body, mesh=mesh, in_specs=(spec,) * 7, out_specs=(spec,) * 4, check_vma=False)
```

```python
import jax
import jax.numpy as jnp
from jax import lax
from jax.experimental import pallas as pl
from jax.experimental.pallas import tpu as pltpu
from jax.sharding import PartitionSpec as P

D = 2880
HS = 360
TOK = 64
FLIGHT = 4
NX = 4
NZ = 8
HALF = 1408
WIDE = D - HALF
CHUNKS = ((0, 512), (512, 1024), (1024, WIDE))
ORDER = (0, 4, 1, 5, 2, 6, 3, 7)
LAG = 3
NCH = len(CHUNKS)
MESH = pl.DeviceIdType.MESH
F32 = jnp.float32
BF16 = jnp.bfloat16


def nt(left, right):
    return lax.dot_general(left, right, (((1,), (1,)), ((), ())), preferred_element_type=F32)


def nn(left, right):
    return jnp.dot(left, right, preferred_element_type=F32)


def selector(ids, rows, per_expert):
    row = lax.broadcasted_iota(jnp.int32, (rows, TOK), 0)
    owner = row // per_expert
    matches = [ids[k : k + 1, :] == owner for k in range(4)]
    hit = matches[0] | matches[1] | matches[2] | matches[3]
    before = lax.broadcasted_iota(jnp.int32, (TOK, TOK), 0)
    token = lax.broadcasted_iota(jnp.int32, (TOK, TOK), 1)
    earlier = jnp.where(before < token, 1.0, 0.0).astype(BF16)
    rank = nn(jnp.where(hit, 1.0, 0.0).astype(BF16), earlier)
    return jnp.where(hit & (rank == (row % 4).astype(F32)), 1.0, 0.0), matches, row % 8 < 4


def kernel(x_hbm, g_hbm, ids_hbm, pr_hbm, wg_hbm, wu_hbm, wd_hbm, *refs):
    gg_o, gu_o, gd_o, sel_o = refs[:4]
    f_o = refs[4 : 4 + NCH]
    refs = refs[4 + NCH :]
    q1s, ts, hs = (refs[j * NCH : (j + 1) * NCH] for j in range(3))
    (
        x_v, g_v, ids_v, ids2_v, pr_v, wg_v, wu_v, wd_v, send_v, rows_v, part_v,
        lsem, sem_z, sem_p, sem_x, sem_f, sem_r, sem_ids, s1, r1, s2, r2,
    ) = refs[3 * NCH :]
    pipe = lax.axis_index("pipe")
    me = lax.axis_index("expert")
    z = lax.div(me, NX)
    x = lax.rem(me, NX)
    xr = lax.rem(x + 1, NX)
    xl = lax.rem(x + NX - 1, NX)
    xo = lax.rem(x + 2, NX)

    def same(zz, xx):
        return {"pipe": pipe, "expert": zz * NX + xx}

    loads = [
        pltpu.make_async_copy(src.at[0], dst, lsem.at[i])
        for i, (src, dst) in enumerate(
            (
                (ids_hbm, ids_v),
                (pr_hbm, pr_v),
                (x_hbm, x_v),
                (g_hbm, g_v),
                (wg_hbm, wg_v),
                (wu_hbm, wu_v),
                (wd_hbm, wd_v),
            )
        )
    ]
    for load in loads:
        load.start()

    barrier = pltpu.get_barrier_semaphore()
    for d in range(1, NZ):
        pl.semaphore_signal(barrier, 1, device_id=same(lax.rem(z + d, NZ), x), device_id_type=MESH)
    t = 2 * lax.rem(z, 2) - 1
    pair = z - t
    for xn in (xl, xr, xo):
        pl.semaphore_signal(barrier, 1, device_id=same(z, xn), device_id_type=MESH)
        pl.semaphore_signal(barrier, 1, device_id=same(pair, xn), device_id_type=MESH)

    def column(shift, steps):
        zz = lax.rem(z + t * steps + NZ, NZ)
        return {"pipe": pipe + shift, "expert": zz * NX + x}

    @pl.when(pipe > 0)
    def _():
        for steps in (0, 1, 2, 3):
            pl.semaphore_signal(barrier, 1, device_id=column(-1, steps), device_id_type=MESH)

    @pl.when(pipe < 7)
    def _():
        for steps in (0, 1, -2, 3):
            pl.semaphore_signal(barrier, 1, device_id=column(1, steps), device_id_type=MESH)

    loads[0].wait()
    loads[1].wait()
    ids = ids_v[...]
    sel, matches, is_in = selector(ids, 32, 8)
    probs = pr_v[...]
    weight = jnp.zeros((32, TOK), F32)
    for k in range(4):
        weight = weight + jnp.where(matches[k], probs[k : k + 1, :], 0.0)
    weight_col = jnp.sum(weight * sel, axis=1, keepdims=True)
    sel_in = jnp.where(is_in, sel, 0.0).astype(BF16)
    sel_co = jnp.where(is_in, 0.0, sel).astype(BF16)
    loads[2].wait()
    loads[3].wait()
    picked = nn(sel_in, x_v[...]) + nn(sel_co, g_v[...]) * weight_col
    send_v[...] = picked.reshape(FLIGHT, 8, D).astype(BF16)

    pl.semaphore_wait(barrier, jnp.where((pipe == 0) | (pipe == 7), 17, 21))

    odd = lax.rem(z, 2)

    def slot(parity, i):
        return (3 - i) + parity * (1 + 2 * i)

    def place(i):
        return slot(odd, i) if i < 4 else slot(1 - odd, i - 4)

    def arrived(xs, i):
        b = (xs, place(i))
        return pltpu.make_async_remote_copy(
            rows_v.at[b], rows_v.at[b], sem_z.at[0], sem_r.at[b],
            device_id=same(z, xr), device_id_type=MESH,
        )

    sends = []

    def send(src, at, to, sem):
        sends.append(
            pltpu.make_async_remote_copy(
                src, rows_v.at[at], sem, sem_r.at[at], device_id=to, device_id_type=MESH
            )
        )
        sends[-1].start()

    def push(i):
        src = send_v.at[lax.div(z, 2)] if i == 0 else rows_v.at[x, place(i)]
        if i < 4:
            send(src, (x, place(i)), same(pair, x), sem_p.at[i])
        send(src, (x, place(i)), same(z, xr), sem_x.at[0, i])
        send(src, (x, place(i)), same(z, xl), sem_x.at[1, i])

    def forward(n, i):
        arrived(xl, i).wait_recv()
        arrived(xr, i).wait_recv()
        here, to = (xl, xr) if n % 2 == 0 else (xr, xl)
        send(rows_v.at[here, place(i)], (here, place(i)), same(z, to), sem_f.at[i])

    push(0)
    for j, step in enumerate((t, -2 * t, 3 * t)):
        zt = lax.rem(z + step + NZ, NZ)
        parity = odd if j == 1 else 1 - odd
        send(send_v.at[lax.div(zt, 2)], (x, slot(parity, j + 1)), same(zt, x), sem_z.at[j])
    own = pltpu.make_async_copy(send_v.at[lax.div(z, 2)], rows_v.at[x, place(0)], sem_r.at[x, place(0)])
    own.start()

    @pl.when(pipe > 0)
    def _():
        pltpu.make_async_remote_copy(
            ids_v, ids2_v, sem_ids.at[0], sem_ids.at[1],
            device_id={"pipe": pipe - 1, "expert": me}, device_id_type=MESH,
        ).start()

    for n, i in enumerate(ORDER):
        if i > 0:
            arrived(x, i).wait_recv()
            push(i)
        if n >= LAG:
            forward(n - LAG, ORDER[n - LAG])
    for n in range(NZ - LAG, NZ):
        forward(n, ORDER[n])
    own.wait()
    for load in loads[4:]:
        load.wait()
    for i in ORDER:
        arrived(xo, i).wait_recv()

    rows = rows_v[...].reshape(256, D)
    pre_gate = nt(wg_v[...], rows)
    pre_up = nt(wu_v[...], rows)
    hidden_grad = pltpu.roll(nt(wd_v[...], rows), 252, 1)
    in_col = lax.broadcasted_iota(jnp.int32, (HS, 256), 1) % 8 < 4
    sigma = jax.nn.sigmoid(pre_gate)
    silu = pre_gate * sigma
    slope = sigma * (1.0 + pre_gate * (1.0 - sigma))
    hidden = jnp.where(in_col, silu * pre_up, 0.0)
    d_gate = jnp.where(in_col, hidden_grad * pre_up * slope, 0.0)
    d_up = jnp.where(in_col, hidden_grad * silu, 0.0)
    hidden_co = pltpu.roll(hidden, 4, 1).astype(BF16)
    gate_lo = d_gate.T.astype(BF16)
    up_lo = d_up.T.astype(BF16)
    gate_hi = pltpu.roll(d_gate, 4, 1).T.astype(BF16)
    up_hi = pltpu.roll(d_up, 4, 1).T.astype(BF16)
    d_gate = d_gate.astype(BF16)
    d_up = d_up.astype(BF16)

    group = lax.div(z, 2)
    members = [(xn, flip) for xn, flip in ((xo, 1), (xo, 0), (xr, 1), (xl, 1), (xr, 0), (xl, 0), (x, 1))]

    def step1(k, j, xn, flip):
        c0, c1 = CHUNKS[k]
        half = odd + flip - 2 * odd * flip
        return pltpu.make_async_remote_copy(
            part_v.at[xn, half, :, pl.ds(c0, c1 - c0)], q1s[k].at[x, odd], s1.at[k, j], r1.at[k, x, odd],
            device_id=same(pair if flip else z, xn), device_id_type=MESH,
        )

    def step2(k, r):
        zt = lax.rem(2 * group - 3 + 4 * odd + r + NZ, NZ)
        return pltpu.make_async_remote_copy(
            ts[k].at[r], hs[k].at[group], s2.at[k, r], r2.at[k, group],
            device_id={"pipe": pipe - 1, "expert": zt * NX + x}, device_id_type=MESH,
        )

    def partials(k):
        c0, c1 = CHUNKS[k]
        lo1 = min(c1, HALF)
        low = nn(gate_lo, wg_v[:, c0:lo1]) + nn(up_lo, wu_v[:, c0:lo1])
        high = nn(gate_hi, wg_v[:, HALF + c0 : HALF + c1]) + nn(up_hi, wu_v[:, HALF + c0 : HALF + c1])
        part_v[:, :, :, c0:lo1] = (low + high[:, : lo1 - c0]).astype(BF16).reshape(NX, 2, 32, lo1 - c0)
        if c1 > lo1:
            part_v[:, :, :, lo1:c1] = high[:, lo1 - c0 :].astype(BF16).reshape(NX, 2, 32, c1 - lo1)
        for j, (xn, flip) in enumerate(members):
            step1(k, j, xn, flip).start()

    def across(k):
        c0, c1 = CHUNKS[k]
        total = part_v[x, odd, :, c0:c1].astype(F32)
        for xn, flip in reversed(members):
            half = odd + flip - 2 * odd * flip
            pltpu.make_async_remote_copy(
                part_v.at[x, odd, :, pl.ds(c0, c1 - c0)], q1s[k].at[xn, half], s1.at[k, 0], r1.at[k, xn, half],
                device_id=same(pair, xn), device_id_type=MESH,
            ).wait_recv()
            total = total + q1s[k][xn, half].astype(F32)
        ts[k][...] = total.reshape(4, 8, c1 - c0).astype(BF16)

        @pl.when(pipe > 0)
        def _():
            for r in range(4):
                step2(k, r).start()

    def grads(left, out):
        out[0] = nn(left, rows_v[...].reshape(256, D)).astype(BF16)

    for k in range(NCH):
        partials(k)
    grads(hidden_co, gd_o)

    @pl.when(pipe == 7)
    def _():
        sel_o[...] = jnp.zeros_like(sel_o)
        for k in range(NCH):
            f_o[k][...] = jnp.zeros_like(f_o[k])

    @pl.when(pipe < 7)
    def _():
        pltpu.make_async_remote_copy(
            ids_v, ids2_v, sem_ids.at[0], sem_ids.at[1],
            device_id={"pipe": pipe, "expert": me}, device_id_type=MESH,
        ).wait_recv()
        sel2, _, low_half = selector(ids2_v[...], 32, 8)
        sel_o[0] = jnp.where(low_half, sel2, 0.0).T.astype(BF16)
        sel_o[1] = jnp.where(low_half, 0.0, sel2).T.astype(BF16)

    grads(d_gate, gg_o)
    across(0)
    grads(d_up, gu_o)
    for k in range(1, NCH):
        across(k)

    @pl.when(pipe < 7)
    def _():
        for k in range(NCH):
            for e in range(FLIGHT):
                pltpu.make_async_remote_copy(
                    ts[k].at[0], hs[k].at[e], s2.at[k, 0], r2.at[k, e],
                    device_id={"pipe": pipe, "expert": me}, device_id_type=MESH,
                ).wait_recv()
            f_o[k][...] = hs[k][...].reshape(f_o[k].shape)

    for copy in sends:
        copy.wait_send()
    for k in range(NCH):
        for j, (xn, flip) in enumerate(members):
            step1(k, j, xn, flip).wait_send()

    @pl.when(pipe > 0)
    def _():
        pltpu.make_async_remote_copy(
            ids_v, ids2_v, sem_ids.at[0], sem_ids.at[1],
            device_id={"pipe": pipe - 1, "expert": me}, device_id_type=MESH,
        ).wait_send()
        for k in range(NCH):
            for r in range(4):
                step2(k, r).wait_send()


def finish(gg_i, gu_i, gd_i, sel_i, *refs):
    f_i = refs[:NCH]
    gg_hbm, gu_hbm, gd_hbm, gp_hbm, gp_v, sem = refs[NCH:]
    copies = [
        pltpu.make_async_copy(src, dst, sem.at[i])
        for i, (src, dst) in enumerate(((gg_i, gg_hbm), (gu_i, gu_hbm), (gd_i, gd_hbm), (gp_v, gp_hbm)))
    ]
    for copy in copies[:3]:
        copy.start()
    for k, (c0, c1) in enumerate(CHUNKS):
        lo1 = min(c1, HALF)
        got = f_i[k][...]
        gp_v[0, :, c0:lo1] = nn(sel_i[0], got[:, : lo1 - c0]).astype(BF16)
        gp_v[0, :, HALF + c0 : HALF + c1] = nn(sel_i[1], got).astype(BF16)
    copies[3].start()
    for copy in copies:
        copy.wait()


def hbm(value):
    return pltpu.with_memory_space_constraint(value, pltpu.HBM)


def body(layer_input, grad_output, expert_ids, gate_probs, w_gate, w_up, w_down):
    ids = jnp.transpose(expert_ids, (0, 2, 1))
    probs = jnp.transpose(gate_probs, (0, 2, 1))
    dma = pltpu.SemaphoreType.DMA
    widths = [c1 - c0 for c0, c1 in CHUNKS]
    wide = (HS, D)
    vmem = pl.BlockSpec(memory_space=pltpu.VMEM)
    anywhere = pl.BlockSpec(memory_space=pl.ANY)
    made = pl.pallas_call(
        kernel,
        out_shape=[pltpu.VMEM((1, HS, D), BF16)] * 3
        + [pltpu.VMEM((2, 64, 32), BF16)]
        + [pltpu.VMEM((32, w), BF16) for w in widths],
        in_specs=[anywhere] * 7,
        out_specs=[vmem] * (4 + NCH),
        scratch_shapes=[pltpu.VMEM((NX, 2, 32, w), BF16) for w in widths]
        + [pltpu.VMEM((FLIGHT, 8, w), BF16) for w in widths] * 2
        + [
            pltpu.VMEM((TOK, D), BF16),
            pltpu.VMEM((TOK, D), BF16),
            pltpu.VMEM((4, TOK), jnp.int32),
            pltpu.VMEM((4, TOK), jnp.int32),
            pltpu.VMEM((4, TOK), F32),
            pltpu.VMEM(wide, BF16),
            pltpu.VMEM(wide, BF16),
            pltpu.VMEM(wide, BF16),
            pltpu.VMEM((FLIGHT, 8, D), BF16),
            pltpu.VMEM((NX, NZ, 8, D), BF16),
            pltpu.VMEM((NX, 2, 32, WIDE), BF16),
            dma((7,)),
            dma((3,)),
            dma((4,)),
            dma((2, NZ)),
            dma((NZ,)),
            dma((NX, NZ)),
            dma((2,)),
            dma((NCH, 7)),
            dma((NCH, NX, 2)),
            dma((NCH, 4)),
            dma((NCH, FLIGHT)),
        ],
        compiler_params=pltpu.CompilerParams(
            collective_id=0, has_side_effects=True, vmem_limit_bytes=40 * 1024 * 1024
        ),
    )(*map(hbm, (layer_input, grad_output, ids, probs, w_gate, w_up, w_down)))
    return tuple(
        pl.pallas_call(
            finish,
            out_shape=[jax.ShapeDtypeStruct((1, HS, D), BF16)] * 3 + [jax.ShapeDtypeStruct((1, TOK, D), BF16)],
            in_specs=[vmem] * (4 + NCH),
            out_specs=[anywhere] * 4,
            scratch_shapes=[pltpu.VMEM((1, TOK, D), BF16), dma((4,))],
            compiler_params=pltpu.CompilerParams(vmem_limit_bytes=16 * 1024 * 1024),
        )(*made)
    )


def solution(mesh):
    spec = P("pipe", "expert", None)
    return jax.shard_map(body, mesh=mesh, in_specs=(spec,) * 7, out_specs=(spec,) * 4, check_vma=False)
```

```python
import jax
import jax.numpy as jnp
from jax import lax
from jax.experimental import pallas as pl
from jax.experimental.pallas import tpu as pltpu
from jax.sharding import PartitionSpec as P

D = 2880
HS = 360
TOK = 64
FLIGHT = 4
NX = 4
NZ = 8
HALF = 1408
WIDE = D - HALF
CHUNKS = ((0, 512), (512, 1024), (1024, WIDE))
ORDER = (0, 4, 1, 5, 2, 6, 3, 7)
LAG = 3
GATE = 0
NCH = len(CHUNKS)
MESH = pl.DeviceIdType.MESH
F32 = jnp.float32
BF16 = jnp.bfloat16


def nt(left, right):
    return lax.dot_general(left, right, (((1,), (1,)), ((), ())), preferred_element_type=F32)


def nn(left, right):
    return jnp.dot(left, right, preferred_element_type=F32)


def selector(ids, rows, per_expert):
    row = lax.broadcasted_iota(jnp.int32, (rows, TOK), 0)
    owner = row // per_expert
    matches = [ids[k : k + 1, :] == owner for k in range(4)]
    hit = matches[0] | matches[1] | matches[2] | matches[3]
    before = lax.broadcasted_iota(jnp.int32, (TOK, TOK), 0)
    token = lax.broadcasted_iota(jnp.int32, (TOK, TOK), 1)
    earlier = jnp.where(before < token, 1.0, 0.0).astype(BF16)
    rank = nn(jnp.where(hit, 1.0, 0.0).astype(BF16), earlier)
    return jnp.where(hit & (rank == (row % 4).astype(F32)), 1.0, 0.0), matches, row % 8 < 4


def kernel(x_hbm, g_hbm, ids_hbm, pr_hbm, wg_hbm, wu_hbm, wd_hbm, *refs):
    gg_o, gu_o, gd_o, sel_o = refs[:4]
    f_o = refs[4 : 4 + NCH]
    refs = refs[4 + NCH :]
    q1s, ts, hs = (refs[j * NCH : (j + 1) * NCH] for j in range(3))
    (
        x_v, g_v, ids_v, ids2_v, pr_v, wg_v, wu_v, wd_v, send_v, rows_v, part_v,
        lsem, sem_z, sem_p, sem_x, sem_f, sem_r, sem_ids, s1, r1, s2, r2, gate,
    ) = refs[3 * NCH :]
    pipe = lax.axis_index("pipe")
    me = lax.axis_index("expert")
    z = lax.div(me, NX)
    x = lax.rem(me, NX)
    xr = lax.rem(x + 1, NX)
    xl = lax.rem(x + NX - 1, NX)
    xo = lax.rem(x + 2, NX)

    def same(zz, xx):
        return {"pipe": pipe, "expert": zz * NX + xx}

    loads = [
        pltpu.make_async_copy(src.at[0], dst, lsem.at[i])
        for i, (src, dst) in enumerate(
            (
                (ids_hbm, ids_v),
                (pr_hbm, pr_v),
                (x_hbm, x_v),
                (g_hbm, g_v),
                (wg_hbm, wg_v),
                (wu_hbm, wu_v),
                (wd_hbm, wd_v),
            )
        )
    ]
    for load in loads:
        load.start()

    barrier = pltpu.get_barrier_semaphore()
    for d in range(1, NZ):
        pl.semaphore_signal(barrier, 1, device_id=same(lax.rem(z + d, NZ), x), device_id_type=MESH)
    t = 2 * lax.rem(z, 2) - 1
    pair = z - t
    for xn in (xl, xr, xo):
        pl.semaphore_signal(barrier, 1, device_id=same(z, xn), device_id_type=MESH)
        pl.semaphore_signal(barrier, 1, device_id=same(pair, xn), device_id_type=MESH)

    def column(shift, steps):
        zz = lax.rem(z + t * steps + NZ, NZ)
        return {"pipe": pipe + shift, "expert": zz * NX + x}

    @pl.when(pipe > 0)
    def _():
        for steps in (0, 1, 2, 3):
            pl.semaphore_signal(barrier, 1, device_id=column(-1, steps), device_id_type=MESH)

    @pl.when(pipe < 7)
    def _():
        for steps in (0, 1, -2, 3):
            pl.semaphore_signal(barrier, 1, device_id=column(1, steps), device_id_type=MESH)

    loads[0].wait()
    loads[1].wait()
    ids = ids_v[...]
    sel, matches, is_in = selector(ids, 32, 8)
    probs = pr_v[...]
    weight = jnp.zeros((32, TOK), F32)
    for k in range(4):
        weight = weight + jnp.where(matches[k], probs[k : k + 1, :], 0.0)
    weight_col = jnp.sum(weight * sel, axis=1, keepdims=True)
    sel_in = jnp.where(is_in, sel, 0.0).astype(BF16)
    sel_co = jnp.where(is_in, 0.0, sel).astype(BF16)
    loads[2].wait()
    loads[3].wait()
    picked = nn(sel_in, x_v[...]) + nn(sel_co, g_v[...]) * weight_col
    send_v[...] = picked.reshape(FLIGHT, 8, D).astype(BF16)

    pl.semaphore_wait(barrier, jnp.where((pipe == 0) | (pipe == 7), 17, 21))

    odd = lax.rem(z, 2)

    def slot(parity, i):
        return (3 - i) + parity * (1 + 2 * i)

    def place(i):
        return slot(odd, i) if i < 4 else slot(1 - odd, i - 4)

    def arrived(xs, i):
        b = (xs, place(i))
        return pltpu.make_async_remote_copy(
            rows_v.at[b], rows_v.at[b], sem_z.at[0], sem_r.at[b],
            device_id=same(z, xr), device_id_type=MESH,
        )

    sends = []

    def send(src, at, to, sem):
        sends.append(
            pltpu.make_async_remote_copy(
                src, rows_v.at[at], sem, sem_r.at[at], device_id=to, device_id_type=MESH
            )
        )
        sends[-1].start()

    def push(i):
        src = send_v.at[lax.div(z, 2)] if i == 0 else rows_v.at[x, place(i)]
        if i < 4:
            send(src, (x, place(i)), same(pair, x), sem_p.at[i])
        send(src, (x, place(i)), same(z, xr), sem_x.at[0, i])
        send(src, (x, place(i)), same(z, xl), sem_x.at[1, i])

    def forward(n, i):
        arrived(xl, i).wait_recv()
        arrived(xr, i).wait_recv()
        here, to = (xl, xr) if n % 2 == 0 else (xr, xl)
        send(rows_v.at[here, place(i)], (here, place(i)), same(z, to), sem_f.at[i])

    @pl.when(lax.rem(pipe, 2) == 1)
    def _():
        pl.semaphore_wait(gate, 1)

    push(0)
    for j, step in enumerate((t, -2 * t, 3 * t)):
        zt = lax.rem(z + step + NZ, NZ)
        parity = odd if j == 1 else 1 - odd
        send(send_v.at[lax.div(zt, 2)], (x, slot(parity, j + 1)), same(zt, x), sem_z.at[j])
    own = pltpu.make_async_copy(send_v.at[lax.div(z, 2)], rows_v.at[x, place(0)], sem_r.at[x, place(0)])
    own.start()

    @pl.when(pipe > 0)
    def _():
        pltpu.make_async_remote_copy(
            ids_v, ids2_v, sem_ids.at[0], sem_ids.at[1],
            device_id={"pipe": pipe - 1, "expert": me}, device_id_type=MESH,
        ).start()

    for n, i in enumerate(ORDER):
        if i > 0:
            arrived(x, i).wait_recv()
            push(i)
        if n == GATE:

            @pl.when(lax.rem(pipe, 2) == 0)
            def _():
                pl.semaphore_signal(
                    gate, 1, device_id={"pipe": pipe + 1, "expert": me}, device_id_type=MESH
                )

        if n >= LAG:
            forward(n - LAG, ORDER[n - LAG])
    for n in range(NZ - LAG, NZ):
        forward(n, ORDER[n])
    own.wait()
    for load in loads[4:]:
        load.wait()
    for i in ORDER:
        arrived(xo, i).wait_recv()

    rows = rows_v[...].reshape(256, D)
    pre_gate = nt(wg_v[...], rows)
    pre_up = nt(wu_v[...], rows)
    hidden_grad = pltpu.roll(nt(wd_v[...], rows), 252, 1)
    in_col = lax.broadcasted_iota(jnp.int32, (HS, 256), 1) % 8 < 4
    sigma = jax.nn.sigmoid(pre_gate)
    silu = pre_gate * sigma
    slope = sigma * (1.0 + pre_gate * (1.0 - sigma))
    hidden = jnp.where(in_col, silu * pre_up, 0.0)
    d_gate = jnp.where(in_col, hidden_grad * pre_up * slope, 0.0)
    d_up = jnp.where(in_col, hidden_grad * silu, 0.0)
    hidden_co = pltpu.roll(hidden, 4, 1).astype(BF16)
    gate_lo = d_gate.T.astype(BF16)
    up_lo = d_up.T.astype(BF16)
    gate_hi = pltpu.roll(d_gate, 4, 1).T.astype(BF16)
    up_hi = pltpu.roll(d_up, 4, 1).T.astype(BF16)
    d_gate = d_gate.astype(BF16)
    d_up = d_up.astype(BF16)

    group = lax.div(z, 2)
    members = [(xn, flip) for xn, flip in ((xo, 1), (xo, 0), (xr, 1), (xl, 1), (xr, 0), (xl, 0), (x, 1))]

    def step1(k, j, xn, flip):
        c0, c1 = CHUNKS[k]
        half = odd + flip - 2 * odd * flip
        return pltpu.make_async_remote_copy(
            part_v.at[xn, half, :, pl.ds(c0, c1 - c0)], q1s[k].at[x, odd], s1.at[k, j], r1.at[k, x, odd],
            device_id=same(pair if flip else z, xn), device_id_type=MESH,
        )

    def step2(k, r):
        zt = lax.rem(2 * group - 3 + 4 * odd + r + NZ, NZ)
        return pltpu.make_async_remote_copy(
            ts[k].at[r], hs[k].at[group], s2.at[k, r], r2.at[k, group],
            device_id={"pipe": pipe - 1, "expert": zt * NX + x}, device_id_type=MESH,
        )

    def partials(k):
        c0, c1 = CHUNKS[k]
        lo1 = min(c1, HALF)
        low = nn(gate_lo, wg_v[:, c0:lo1]) + nn(up_lo, wu_v[:, c0:lo1])
        high = nn(gate_hi, wg_v[:, HALF + c0 : HALF + c1]) + nn(up_hi, wu_v[:, HALF + c0 : HALF + c1])
        part_v[:, :, :, c0:lo1] = (low + high[:, : lo1 - c0]).astype(BF16).reshape(NX, 2, 32, lo1 - c0)
        if c1 > lo1:
            part_v[:, :, :, lo1:c1] = high[:, lo1 - c0 :].astype(BF16).reshape(NX, 2, 32, c1 - lo1)
        for j, (xn, flip) in enumerate(members):
            step1(k, j, xn, flip).start()

    def across(k):
        c0, c1 = CHUNKS[k]
        total = part_v[x, odd, :, c0:c1].astype(F32)
        for xn, flip in reversed(members):
            half = odd + flip - 2 * odd * flip
            pltpu.make_async_remote_copy(
                part_v.at[x, odd, :, pl.ds(c0, c1 - c0)], q1s[k].at[xn, half], s1.at[k, 0], r1.at[k, xn, half],
                device_id=same(pair, xn), device_id_type=MESH,
            ).wait_recv()
            total = total + q1s[k][xn, half].astype(F32)
        ts[k][...] = total.reshape(4, 8, c1 - c0).astype(BF16)

        @pl.when(pipe > 0)
        def _():
            for r in range(4):
                step2(k, r).start()

    def grads(left, out):
        out[0] = nn(left, rows_v[...].reshape(256, D)).astype(BF16)

    for k in range(NCH):
        partials(k)
    grads(hidden_co, gd_o)

    @pl.when(pipe == 7)
    def _():
        sel_o[...] = jnp.zeros_like(sel_o)
        for k in range(NCH):
            f_o[k][...] = jnp.zeros_like(f_o[k])

    @pl.when(pipe < 7)
    def _():
        pltpu.make_async_remote_copy(
            ids_v, ids2_v, sem_ids.at[0], sem_ids.at[1],
            device_id={"pipe": pipe, "expert": me}, device_id_type=MESH,
        ).wait_recv()
        sel2, _, low_half = selector(ids2_v[...], 32, 8)
        sel_o[0] = jnp.where(low_half, sel2, 0.0).T.astype(BF16)
        sel_o[1] = jnp.where(low_half, 0.0, sel2).T.astype(BF16)

    across(0)
    grads(d_gate, gg_o)
    across(1)
    grads(d_up, gu_o)
    for k in range(2, NCH):
        across(k)

    @pl.when(pipe < 7)
    def _():
        for k in range(NCH):
            for e in range(FLIGHT):
                pltpu.make_async_remote_copy(
                    ts[k].at[0], hs[k].at[e], s2.at[k, 0], r2.at[k, e],
                    device_id={"pipe": pipe, "expert": me}, device_id_type=MESH,
                ).wait_recv()
            f_o[k][...] = hs[k][...].reshape(f_o[k].shape)

    for copy in sends:
        copy.wait_send()
    for k in range(NCH):
        for j, (xn, flip) in enumerate(members):
            step1(k, j, xn, flip).wait_send()

    @pl.when(pipe > 0)
    def _():
        pltpu.make_async_remote_copy(
            ids_v, ids2_v, sem_ids.at[0], sem_ids.at[1],
            device_id={"pipe": pipe - 1, "expert": me}, device_id_type=MESH,
        ).wait_send()
        for k in range(NCH):
            for r in range(4):
                step2(k, r).wait_send()


def finish(gg_i, gu_i, gd_i, sel_i, *refs):
    f_i = refs[:NCH]
    gg_hbm, gu_hbm, gd_hbm, gp_hbm, gp_v, sem = refs[NCH:]
    copies = [
        pltpu.make_async_copy(src, dst, sem.at[i])
        for i, (src, dst) in enumerate(((gg_i, gg_hbm), (gu_i, gu_hbm), (gd_i, gd_hbm), (gp_v, gp_hbm)))
    ]
    for copy in copies[:3]:
        copy.start()
    for k, (c0, c1) in enumerate(CHUNKS):
        lo1 = min(c1, HALF)
        got = f_i[k][...]
        gp_v[0, :, c0:lo1] = nn(sel_i[0], got[:, : lo1 - c0]).astype(BF16)
        gp_v[0, :, HALF + c0 : HALF + c1] = nn(sel_i[1], got).astype(BF16)
    copies[3].start()
    for copy in copies:
        copy.wait()


def hbm(value):
    return pltpu.with_memory_space_constraint(value, pltpu.HBM)


def body(layer_input, grad_output, expert_ids, gate_probs, w_gate, w_up, w_down):
    ids = jnp.transpose(expert_ids, (0, 2, 1))
    probs = jnp.transpose(gate_probs, (0, 2, 1))
    dma = pltpu.SemaphoreType.DMA
    widths = [c1 - c0 for c0, c1 in CHUNKS]
    wide = (HS, D)
    vmem = pl.BlockSpec(memory_space=pltpu.VMEM)
    anywhere = pl.BlockSpec(memory_space=pl.ANY)
    made = pl.pallas_call(
        kernel,
        out_shape=[pltpu.VMEM((1, HS, D), BF16)] * 3
        + [pltpu.VMEM((2, 64, 32), BF16)]
        + [pltpu.VMEM((32, w), BF16) for w in widths],
        in_specs=[anywhere] * 7,
        out_specs=[vmem] * (4 + NCH),
        scratch_shapes=[pltpu.VMEM((NX, 2, 32, w), BF16) for w in widths]
        + [pltpu.VMEM((FLIGHT, 8, w), BF16) for w in widths] * 2
        + [
            pltpu.VMEM((TOK, D), BF16),
            pltpu.VMEM((TOK, D), BF16),
            pltpu.VMEM((4, TOK), jnp.int32),
            pltpu.VMEM((4, TOK), jnp.int32),
            pltpu.VMEM((4, TOK), F32),
            pltpu.VMEM(wide, BF16),
            pltpu.VMEM(wide, BF16),
            pltpu.VMEM(wide, BF16),
            pltpu.VMEM((FLIGHT, 8, D), BF16),
            pltpu.VMEM((NX, NZ, 8, D), BF16),
            pltpu.VMEM((NX, 2, 32, WIDE), BF16),
            dma((7,)),
            dma((3,)),
            dma((4,)),
            dma((2, NZ)),
            dma((NZ,)),
            dma((NX, NZ)),
            dma((2,)),
            dma((NCH, 7)),
            dma((NCH, NX, 2)),
            dma((NCH, 4)),
            dma((NCH, FLIGHT)),
            pltpu.SemaphoreType.REGULAR,
        ],
        compiler_params=pltpu.CompilerParams(
            collective_id=0, has_side_effects=True, vmem_limit_bytes=40 * 1024 * 1024
        ),
    )(*map(hbm, (layer_input, grad_output, ids, probs, w_gate, w_up, w_down)))
    return tuple(
        pl.pallas_call(
            finish,
            out_shape=[jax.ShapeDtypeStruct((1, HS, D), BF16)] * 3 + [jax.ShapeDtypeStruct((1, TOK, D), BF16)],
            in_specs=[vmem] * (4 + NCH),
            out_specs=[anywhere] * 4,
            scratch_shapes=[pltpu.VMEM((1, TOK, D), BF16), dma((4,))],
            compiler_params=pltpu.CompilerParams(vmem_limit_bytes=16 * 1024 * 1024),
        )(*made)
    )


def solution(mesh):
    spec = P("pipe", "expert", None)
    return jax.shard_map(body, mesh=mesh, in_specs=(spec,) * 7, out_specs=(spec,) * 4, check_vma=False)
```

```python
import jax
import jax.numpy as jnp
from jax import lax
from jax.experimental import pallas as pl
from jax.experimental.pallas import tpu as pltpu
from jax.sharding import PartitionSpec as P

D = 2880
HS = 360
TOK = 64
FLIGHT = 4
NX = 4
NZ = 8
HALF = 1408
WIDE = D - HALF
CHUNKS = ((0, 512), (512, 1024), (1024, WIDE))
ORDER = (0, 1, 4, 2, 5, 3, 6, 7)
LAG = 3
GATE = 0
NCH = len(CHUNKS)
MESH = pl.DeviceIdType.MESH
F32 = jnp.float32
BF16 = jnp.bfloat16


def nt(left, right):
    return lax.dot_general(left, right, (((1,), (1,)), ((), ())), preferred_element_type=F32)


def nn(left, right):
    return jnp.dot(left, right, preferred_element_type=F32)


def selector(ids, rows, per_expert):
    row = lax.broadcasted_iota(jnp.int32, (rows, TOK), 0)
    owner = row // per_expert
    matches = [ids[k : k + 1, :] == owner for k in range(4)]
    hit = matches[0] | matches[1] | matches[2] | matches[3]
    before = lax.broadcasted_iota(jnp.int32, (TOK, TOK), 0)
    token = lax.broadcasted_iota(jnp.int32, (TOK, TOK), 1)
    earlier = jnp.where(before < token, 1.0, 0.0).astype(BF16)
    rank = nn(jnp.where(hit, 1.0, 0.0).astype(BF16), earlier)
    return jnp.where(hit & (rank == (row % 4).astype(F32)), 1.0, 0.0), matches, row % 8 < 4


def kernel(x_hbm, g_hbm, ids_hbm, pr_hbm, wg_hbm, wu_hbm, wd_hbm, *refs):
    gg_o, gu_o, gd_o, sel_o = refs[:4]
    f_o = refs[4 : 4 + NCH]
    refs = refs[4 + NCH :]
    q1s, ts, hs = (refs[j * NCH : (j + 1) * NCH] for j in range(3))
    (
        x_v, g_v, ids_v, ids2_v, pr_v, wg_v, wu_v, wd_v, send_v, rows_v, part_v,
        lsem, sem_z, sem_p, sem_x, sem_f, sem_r, sem_ids, s1, r1, s2, r2, gate,
    ) = refs[3 * NCH :]
    pipe = lax.axis_index("pipe")
    me = lax.axis_index("expert")
    z = lax.div(me, NX)
    x = lax.rem(me, NX)
    xr = lax.rem(x + 1, NX)
    xl = lax.rem(x + NX - 1, NX)
    xo = lax.rem(x + 2, NX)

    def same(zz, xx):
        return {"pipe": pipe, "expert": zz * NX + xx}

    loads = [
        pltpu.make_async_copy(src.at[0], dst, lsem.at[i])
        for i, (src, dst) in enumerate(
            (
                (ids_hbm, ids_v),
                (pr_hbm, pr_v),
                (x_hbm, x_v),
                (g_hbm, g_v),
                (wg_hbm, wg_v),
                (wu_hbm, wu_v),
                (wd_hbm, wd_v),
            )
        )
    ]
    for load in loads:
        load.start()

    barrier = pltpu.get_barrier_semaphore()
    for d in range(1, NZ):
        pl.semaphore_signal(barrier, 1, device_id=same(lax.rem(z + d, NZ), x), device_id_type=MESH)
    t = 2 * lax.rem(z, 2) - 1
    pair = z - t
    for xn in (xl, xr, xo):
        pl.semaphore_signal(barrier, 1, device_id=same(z, xn), device_id_type=MESH)
        pl.semaphore_signal(barrier, 1, device_id=same(pair, xn), device_id_type=MESH)

    def column(shift, steps):
        zz = lax.rem(z + t * steps + NZ, NZ)
        return {"pipe": pipe + shift, "expert": zz * NX + x}

    @pl.when(pipe > 0)
    def _():
        for steps in (0, 1, 2, 3):
            pl.semaphore_signal(barrier, 1, device_id=column(-1, steps), device_id_type=MESH)

    @pl.when(pipe < 7)
    def _():
        for steps in (0, 1, -2, 3):
            pl.semaphore_signal(barrier, 1, device_id=column(1, steps), device_id_type=MESH)

    loads[0].wait()
    loads[1].wait()
    ids = ids_v[...]
    sel, matches, is_in = selector(ids, 32, 8)
    probs = pr_v[...]
    weight = jnp.zeros((32, TOK), F32)
    for k in range(4):
        weight = weight + jnp.where(matches[k], probs[k : k + 1, :], 0.0)
    weight_col = jnp.sum(weight * sel, axis=1, keepdims=True)
    sel_in = jnp.where(is_in, sel, 0.0).astype(BF16)
    sel_co = jnp.where(is_in, 0.0, sel).astype(BF16)
    loads[2].wait()
    loads[3].wait()
    picked = nn(sel_in, x_v[...]) + nn(sel_co, g_v[...]) * weight_col
    send_v[...] = picked.reshape(FLIGHT, 8, D).astype(BF16)

    pl.semaphore_wait(barrier, jnp.where((pipe == 0) | (pipe == 7), 17, 21))

    odd = lax.rem(z, 2)

    def slot(parity, i):
        return (3 - i) + parity * (1 + 2 * i)

    def place(i):
        return slot(odd, i) if i < 4 else slot(1 - odd, i - 4)

    def arrived(xs, i):
        b = (xs, place(i))
        return pltpu.make_async_remote_copy(
            rows_v.at[b], rows_v.at[b], sem_z.at[0], sem_r.at[b],
            device_id=same(z, xr), device_id_type=MESH,
        )

    sends = []

    def send(src, at, to, sem):
        sends.append(
            pltpu.make_async_remote_copy(
                src, rows_v.at[at], sem, sem_r.at[at], device_id=to, device_id_type=MESH
            )
        )
        sends[-1].start()

    def push(i):
        src = send_v.at[lax.div(z, 2)] if i == 0 else rows_v.at[x, place(i)]
        send(src, (x, place(i)), same(z, xr), sem_x.at[0, i])
        send(src, (x, place(i)), same(z, xl), sem_x.at[1, i])
        if i < 4:
            send(src, (x, place(i)), same(pair, x), sem_p.at[i])

    def forward(n, i):
        arrived(xl, i).wait_recv()
        arrived(xr, i).wait_recv()
        here, to = (xl, xr) if n % 2 == 0 else (xr, xl)
        send(rows_v.at[here, place(i)], (here, place(i)), same(z, to), sem_f.at[i])

    @pl.when(lax.rem(pipe, 2) == 1)
    def _():
        pl.semaphore_wait(gate, 1)

    push(0)
    for j, step in enumerate((t, -2 * t, 3 * t)):
        zt = lax.rem(z + step + NZ, NZ)
        parity = odd if j == 1 else 1 - odd
        send(send_v.at[lax.div(zt, 2)], (x, slot(parity, j + 1)), same(zt, x), sem_z.at[j])
    own = pltpu.make_async_copy(send_v.at[lax.div(z, 2)], rows_v.at[x, place(0)], sem_r.at[x, place(0)])
    own.start()

    @pl.when(pipe > 0)
    def _():
        pltpu.make_async_remote_copy(
            ids_v, ids2_v, sem_ids.at[0], sem_ids.at[1],
            device_id={"pipe": pipe - 1, "expert": me}, device_id_type=MESH,
        ).start()

    for n, i in enumerate(ORDER):
        if i > 0:
            arrived(x, i).wait_recv()
            push(i)
        if n == GATE:

            @pl.when(lax.rem(pipe, 2) == 0)
            def _():
                pl.semaphore_signal(
                    gate, 1, device_id={"pipe": pipe + 1, "expert": me}, device_id_type=MESH
                )

        if n >= LAG:
            forward(n - LAG, ORDER[n - LAG])
    for n in range(NZ - LAG, NZ):
        forward(n, ORDER[n])
    own.wait()
    for load in loads[4:]:
        load.wait()
    for i in ORDER:
        arrived(xo, i).wait_recv()

    rows = rows_v[...].reshape(256, D)
    pre_gate = nt(wg_v[...], rows)
    pre_up = nt(wu_v[...], rows)
    hidden_grad = pltpu.roll(nt(wd_v[...], rows), 252, 1)
    in_col = lax.broadcasted_iota(jnp.int32, (HS, 256), 1) % 8 < 4
    sigma = jax.nn.sigmoid(pre_gate)
    silu = pre_gate * sigma
    slope = sigma * (1.0 + pre_gate * (1.0 - sigma))
    hidden = jnp.where(in_col, silu * pre_up, 0.0)
    d_gate = jnp.where(in_col, hidden_grad * pre_up * slope, 0.0)
    d_up = jnp.where(in_col, hidden_grad * silu, 0.0)
    hidden_co = pltpu.roll(hidden, 4, 1).astype(BF16)
    gate_lo = d_gate.T.astype(BF16)
    up_lo = d_up.T.astype(BF16)
    gate_hi = pltpu.roll(d_gate, 4, 1).T.astype(BF16)
    up_hi = pltpu.roll(d_up, 4, 1).T.astype(BF16)
    d_gate = d_gate.astype(BF16)
    d_up = d_up.astype(BF16)

    group = lax.div(z, 2)
    members = [(xn, flip) for xn, flip in ((xo, 1), (xo, 0), (xr, 1), (xl, 1), (xr, 0), (xl, 0), (x, 1))]

    def step1(k, j, xn, flip):
        c0, c1 = CHUNKS[k]
        half = odd + flip - 2 * odd * flip
        return pltpu.make_async_remote_copy(
            part_v.at[xn, half, :, pl.ds(c0, c1 - c0)], q1s[k].at[x, odd], s1.at[k, j], r1.at[k, x, odd],
            device_id=same(pair if flip else z, xn), device_id_type=MESH,
        )

    def step2(k, r):
        zt = lax.rem(2 * group - 3 + 4 * odd + r + NZ, NZ)
        return pltpu.make_async_remote_copy(
            ts[k].at[r], hs[k].at[group], s2.at[k, r], r2.at[k, group],
            device_id={"pipe": pipe - 1, "expert": zt * NX + x}, device_id_type=MESH,
        )

    def partials(k):
        c0, c1 = CHUNKS[k]
        lo1 = min(c1, HALF)
        low = nn(gate_lo, wg_v[:, c0:lo1]) + nn(up_lo, wu_v[:, c0:lo1])
        high = nn(gate_hi, wg_v[:, HALF + c0 : HALF + c1]) + nn(up_hi, wu_v[:, HALF + c0 : HALF + c1])
        part_v[:, :, :, c0:lo1] = (low + high[:, : lo1 - c0]).astype(BF16).reshape(NX, 2, 32, lo1 - c0)
        if c1 > lo1:
            part_v[:, :, :, lo1:c1] = high[:, lo1 - c0 :].astype(BF16).reshape(NX, 2, 32, c1 - lo1)
        for j, (xn, flip) in enumerate(members):
            step1(k, j, xn, flip).start()

    def across(k):
        c0, c1 = CHUNKS[k]
        total = part_v[x, odd, :, c0:c1].astype(F32)
        for xn, flip in reversed(members):
            half = odd + flip - 2 * odd * flip
            pltpu.make_async_remote_copy(
                part_v.at[x, odd, :, pl.ds(c0, c1 - c0)], q1s[k].at[xn, half], s1.at[k, 0], r1.at[k, xn, half],
                device_id=same(pair, xn), device_id_type=MESH,
            ).wait_recv()
            total = total + q1s[k][xn, half].astype(F32)
        ts[k][...] = total.reshape(4, 8, c1 - c0).astype(BF16)

        @pl.when(pipe > 0)
        def _():
            for r in range(4):
                step2(k, r).start()

    def grads(left, out):
        out[0] = nn(left, rows_v[...].reshape(256, D)).astype(BF16)

    for k in range(NCH):
        partials(k)
    grads(hidden_co, gd_o)

    @pl.when(pipe == 7)
    def _():
        sel_o[...] = jnp.zeros_like(sel_o)
        for k in range(NCH):
            f_o[k][...] = jnp.zeros_like(f_o[k])

    @pl.when(pipe < 7)
    def _():
        pltpu.make_async_remote_copy(
            ids_v, ids2_v, sem_ids.at[0], sem_ids.at[1],
            device_id={"pipe": pipe, "expert": me}, device_id_type=MESH,
        ).wait_recv()
        sel2, _, low_half = selector(ids2_v[...], 32, 8)
        sel_o[0] = jnp.where(low_half, sel2, 0.0).T.astype(BF16)
        sel_o[1] = jnp.where(low_half, 0.0, sel2).T.astype(BF16)

    across(0)
    grads(d_gate, gg_o)
    across(1)
    grads(d_up, gu_o)
    for k in range(2, NCH):
        across(k)

    @pl.when(pipe < 7)
    def _():
        for k in range(NCH):
            for e in range(FLIGHT):
                pltpu.make_async_remote_copy(
                    ts[k].at[0], hs[k].at[e], s2.at[k, 0], r2.at[k, e],
                    device_id={"pipe": pipe, "expert": me}, device_id_type=MESH,
                ).wait_recv()
            f_o[k][...] = hs[k][...].reshape(f_o[k].shape)

    for copy in sends:
        copy.wait_send()
    for k in range(NCH):
        for j, (xn, flip) in enumerate(members):
            step1(k, j, xn, flip).wait_send()

    @pl.when(pipe > 0)
    def _():
        pltpu.make_async_remote_copy(
            ids_v, ids2_v, sem_ids.at[0], sem_ids.at[1],
            device_id={"pipe": pipe - 1, "expert": me}, device_id_type=MESH,
        ).wait_send()
        for k in range(NCH):
            for r in range(4):
                step2(k, r).wait_send()


def finish(gg_i, gu_i, gd_i, sel_i, *refs):
    f_i = refs[:NCH]
    gg_hbm, gu_hbm, gd_hbm, gp_hbm, gp_v, sem = refs[NCH:]
    copies = [
        pltpu.make_async_copy(src, dst, sem.at[i])
        for i, (src, dst) in enumerate(((gg_i, gg_hbm), (gu_i, gu_hbm), (gd_i, gd_hbm), (gp_v, gp_hbm)))
    ]
    for copy in copies[:3]:
        copy.start()
    for k, (c0, c1) in enumerate(CHUNKS):
        lo1 = min(c1, HALF)
        got = f_i[k][...]
        gp_v[0, :, c0:lo1] = nn(sel_i[0], got[:, : lo1 - c0]).astype(BF16)
        gp_v[0, :, HALF + c0 : HALF + c1] = nn(sel_i[1], got).astype(BF16)
    copies[3].start()
    for copy in copies:
        copy.wait()


def hbm(value):
    return pltpu.with_memory_space_constraint(value, pltpu.HBM)


def body(layer_input, grad_output, expert_ids, gate_probs, w_gate, w_up, w_down):
    ids = jnp.transpose(expert_ids, (0, 2, 1))
    probs = jnp.transpose(gate_probs, (0, 2, 1))
    dma = pltpu.SemaphoreType.DMA
    widths = [c1 - c0 for c0, c1 in CHUNKS]
    wide = (HS, D)
    vmem = pl.BlockSpec(memory_space=pltpu.VMEM)
    anywhere = pl.BlockSpec(memory_space=pl.ANY)
    made = pl.pallas_call(
        kernel,
        out_shape=[pltpu.VMEM((1, HS, D), BF16)] * 3
        + [pltpu.VMEM((2, 64, 32), BF16)]
        + [pltpu.VMEM((32, w), BF16) for w in widths],
        in_specs=[anywhere] * 7,
        out_specs=[vmem] * (4 + NCH),
        scratch_shapes=[pltpu.VMEM((NX, 2, 32, w), BF16) for w in widths]
        + [pltpu.VMEM((FLIGHT, 8, w), BF16) for w in widths] * 2
        + [
            pltpu.VMEM((TOK, D), BF16),
            pltpu.VMEM((TOK, D), BF16),
            pltpu.VMEM((4, TOK), jnp.int32),
            pltpu.VMEM((4, TOK), jnp.int32),
            pltpu.VMEM((4, TOK), F32),
            pltpu.VMEM(wide, BF16),
            pltpu.VMEM(wide, BF16),
            pltpu.VMEM(wide, BF16),
            pltpu.VMEM((FLIGHT, 8, D), BF16),
            pltpu.VMEM((NX, NZ, 8, D), BF16),
            pltpu.VMEM((NX, 2, 32, WIDE), BF16),
            dma((7,)),
            dma((3,)),
            dma((4,)),
            dma((2, NZ)),
            dma((NZ,)),
            dma((NX, NZ)),
            dma((2,)),
            dma((NCH, 7)),
            dma((NCH, NX, 2)),
            dma((NCH, 4)),
            dma((NCH, FLIGHT)),
            pltpu.SemaphoreType.REGULAR,
        ],
        compiler_params=pltpu.CompilerParams(
            collective_id=0, has_side_effects=True, vmem_limit_bytes=40 * 1024 * 1024
        ),
    )(*map(hbm, (layer_input, grad_output, ids, probs, w_gate, w_up, w_down)))
    return tuple(
        pl.pallas_call(
            finish,
            out_shape=[jax.ShapeDtypeStruct((1, HS, D), BF16)] * 3 + [jax.ShapeDtypeStruct((1, TOK, D), BF16)],
            in_specs=[vmem] * (4 + NCH),
            out_specs=[anywhere] * 4,
            scratch_shapes=[pltpu.VMEM((1, TOK, D), BF16), dma((4,))],
            compiler_params=pltpu.CompilerParams(vmem_limit_bytes=16 * 1024 * 1024),
        )(*made)
    )


def solution(mesh):
    spec = P("pipe", "expert", None)
    return jax.shard_map(body, mesh=mesh, in_specs=(spec,) * 7, out_specs=(spec,) * 4, check_vma=False)
```
